32 devices in a mesh: dev: 32 (over z, y, x, core).
Axes of the slice: x: 2, y: 2, z: 4, core: 2. Of those that a mesh axis runs over, the one named last changes fastest.
Arguments:
- fluxes: float32 [32, 49152], P(None, 'dev'), may hold values from -6 to 6
- neighbours: int32 [4, 49152], P(None, 'dev'), may hold values from 0 to 1727, as said below
- grad_coef: float32 [4, 2, 49152], P(None, None, 'dev'), may hold values from -3 to 3
- source_cell: int32 [16, 12288], P(None, 'dev'), may hold values from 0 to 1535
- displacement: float32 [2, 16, 12288], P(None, None, 'dev'), may hold values from -1 to 1
- margin_weight: float32 [16, 12288], P(None, 'dev'), may hold values from 0.05 to 1
- live_count: int32 [32, 16], P('dev'), may hold values from 1 to 384, as said below
- target_cell: int32 [16, 12288], P(None, 'dev'), may hold values from 0 to 767
- ocean_area: float32 [24576], P('dev'), may hold values from 2 to 8
- sea_temp: float32 [24576], P('dev'), may hold values from -6 to 6
- atmos_area: float32 [49152], P('dev'), may hold values from 1 to 4
Outputs:
- ocean_flux: float32 [32, 24576], P(None, 'dev')
- atmos_sst: float32 [49152], P('dev')
The draws below stay inside these ranges and needn't reach their ends.
Inputs may be any that keep to these rules, and one draw needn't show every extreme that they name: A cell's neighbours lie within 96 cells of it along the curve. `live_count`: every device has a full block in some round.
All inputs are finite; a program needn't handle non-finite values.
Results may differ from the reference program's by a relative error of at most 0.00002.
Values sent between devices are 32-bit elements; how exact they have to be, the bound alone decides.
No kernel may reach another device: no remote copies, remote signals or barrier semaphores. Data moves between devices by JAX's collectives and lax.ppermute only.
A program may use at most 64 MiB of HBM per device.

```python
import math
import jax
import jax.numpy as jnp

NBR = 4
PARTNERS = 16
A_DEV = 1536
FIELDS = 32
HALO = 96
SLOT_DEV = 384
O_DEV = 768
NA = 49152
NO = 24576
SLOTS = 12288
N_DEV = 32


def draw_neighbours(key, part):
    shifts = jax.random.randint(key, (NBR, N_DEV, A_DEV), -HALO, HALO + 1, dtype=jnp.int32)
    shifts = shifts.at[0, :, 0].set(-HALO)
    shifts = shifts.at[0, :, A_DEV - 1].set(HALO)
    positions = jnp.arange(A_DEV, dtype=jnp.int32)[None, None, :] + HALO + shifts
    return positions.reshape(NBR, N_DEV * A_DEV)


def draw_live_count(key, part):
    first_key, second_key = jax.random.split(key)
    lowest = jax.random.randint(first_key, (N_DEV, 1), 1, SLOT_DEV // 2 + 1, dtype=jnp.int32)
    counts = jax.random.randint(second_key, (N_DEV, PARTNERS), 0, SLOT_DEV + 1, dtype=jnp.int32)
    counts = jnp.maximum(counts, lowest)
    device_ids = jnp.arange(N_DEV, dtype=jnp.int32)
    return counts.at[device_ids, device_ids % PARTNERS].set(SLOT_DEV)


def place_ends(array, key, least, high):
    longest = array.shape.index(max(array.shape))
    spots = []
    for shift in (0, 1):
        where = [jax.random.randint(jax.random.fold_in(key, axis), (), 0, length) for axis, length in enumerate(array.shape)]
        where[longest] = (where[longest] + shift) % array.shape[longest]
        spots.append(tuple(where))
    return array.at[spots[0]].set(least).at[spots[1]].set(high)


def levels(own_key, extent, shards, low, high):
    def one(axis_at, blocks):
        steps = jax.random.uniform(jax.random.fold_in(jax.random.fold_in(own_key, 6), axis_at), (blocks,), jnp.float32, low / len(shards), high / len(shards))
        return jnp.repeat(jnp.exp(steps), extent[axis_at] // blocks).reshape((-1,) + (1,) * (len(extent) - axis_at - 1))

    loudness = one(*shards[0])
    for cut in shards[1:]:
        loudness = loudness * one(*cut)
    return loudness


def gaussian(stream_key, dims, width, limit, shards=(), kind=jnp.bfloat16):
    level = levels(stream_key, dims, shards, -0.22, 0.18) if shards else 1.0
    drawn = jax.random.normal(stream_key, dims, jnp.float32) * width * level
    return jnp.minimum(jnp.maximum(drawn, -limit), limit).astype(kind)


def setup_inputs(seed: int = 0) -> dict:
    arg_keys = jax.random.split(jax.random.key(seed), 12)
    return {
        "fluxes": gaussian(arg_keys[0], (FIELDS, NA), 1.0, 6.0, ((1, 32),), jnp.float32),
        "neighbours": draw_neighbours(jax.random.fold_in(arg_keys[11], 71), 0),
        "grad_coef": gaussian(arg_keys[2], (NBR, 2, NA), 0.5, 3.0, ((2, 32),), jnp.float32),
        "source_cell": place_ends(jax.random.randint(arg_keys[3], (PARTNERS, SLOTS), 0, A_DEV), jax.random.fold_in(arg_keys[3], 1), 0, A_DEV - 1).astype(jnp.int32),
        "displacement": jnp.clip(jax.random.uniform(arg_keys[4], (2, PARTNERS, SLOTS), jnp.float32, -1.0, 1.0) * levels(arg_keys[4], (2, PARTNERS, SLOTS), ((2, 32),), -0.4, 0.0), -1.0, 1.0),
        "margin_weight": jnp.clip(jnp.exp(math.log(1.0) - 2.9957323 * jax.random.uniform(arg_keys[5], (PARTNERS, SLOTS), jnp.float32) ** levels(arg_keys[5], (PARTNERS, SLOTS), ((1, 32),), -0.2, 0.2)), 0.05, 1.0),
        "live_count": draw_live_count(jax.random.fold_in(arg_keys[11], 71), 0),
        "target_cell": place_ends(jax.random.randint(arg_keys[7], (PARTNERS, SLOTS), 0, O_DEV), jax.random.fold_in(arg_keys[7], 1), 0, O_DEV - 1).astype(jnp.int32),
        "ocean_area": jnp.clip(jnp.exp(math.log(8.0) - 1.3862944 * jax.random.uniform(arg_keys[8], (NO,), jnp.float32) ** levels(arg_keys[8], (NO,), ((0, 32),), -0.2, 0.2)), 2.0, 8.0),
        "sea_temp": gaussian(arg_keys[9], (NO,), 1.0, 6.0, ((0, 32),), jnp.float32),
        "atmos_area": jnp.clip(jnp.exp(math.log(4.0) - 1.3862944 * jax.random.uniform(arg_keys[10], (NA,), jnp.float32) ** levels(arg_keys[10], (NA,), ((0, 32),), -0.2, 0.2)), 1.0, 4.0),
    }


def reference(fluxes, neighbours, grad_coef, source_cell, displacement, margin_weight, live_count, target_cell, ocean_area, sea_temp, atmos_area):
    total_atm = fluxes.shape[1]
    cells = jnp.arange(total_atm, dtype=jnp.int32)
    base_cell = (cells // A_DEV) * A_DEV
    grad_zero = jnp.zeros(fluxes.shape, jnp.float32)
    grad_one = jnp.zeros(fluxes.shape, jnp.float32)
    for nbr_index in range(NBR):
        global_nbr = (base_cell - HALO + neighbours[nbr_index]) % total_atm
        differ = fluxes[:, global_nbr] - fluxes
        grad_zero = grad_zero + grad_coef[nbr_index, 0][None, :] * differ
        grad_one = grad_one + grad_coef[nbr_index, 1][None, :] * differ
    slot_ids = jnp.arange(SLOTS, dtype=jnp.int32)
    slot_dev = slot_ids // SLOT_DEV
    slot_pos = slot_ids % SLOT_DEV
    ocean_acc = jnp.zeros((fluxes.shape[0], O_DEV * N_DEV), jnp.float32)
    atmos_acc = jnp.zeros((total_atm,), jnp.float32)
    for round_index in range(PARTNERS):
        offset = round_index - PARTNERS // 2
        source = slot_dev * A_DEV + source_cell[round_index]
        alive = slot_pos < live_count[slot_dev, round_index]
        weight_live = jnp.where(alive, margin_weight[round_index], jnp.float32(0.0))
        recon = fluxes[:, source] + displacement[0, round_index][None, :] * grad_zero[:, source] + displacement[1, round_index][None, :] * grad_one[:, source]
        target_dev = (slot_dev + offset) % N_DEV
        target = target_dev * O_DEV + target_cell[round_index, target_dev * SLOT_DEV + slot_pos]
        ocean_acc = ocean_acc.at[:, target].add(recon * weight_live[None, :])
        atmos_acc = atmos_acc.at[source].add(sea_temp[target] * weight_live)
    return ocean_acc / ocean_area[None, :], atmos_acc / atmos_area
```

```python
import jax
import jax.numpy as jnp
from jax import lax
from jax.experimental import pallas as pl
from jax.experimental.pallas import tpu as pltpu
from jax.sharding import PartitionSpec as P

HALO = 96
LANES = 128
SUB = 8
WIDE = 256
F32 = jnp.float32
I32 = jnp.int32
BF16 = jnp.bfloat16


def take_lanes(table, lane):
    return jnp.take_along_axis(table, lane, axis=1, mode="promise_in_bounds")


def spread(row, count=SUB):
    return jnp.broadcast_to(row, (count, row.shape[1]))


def on_mxu(a, b):
    return lax.dot_general(a, b, (((1,), (1,)), ((), ())), preferred_element_type=F32)


def halves(x):
    high = x.astype(BF16)
    return high, (x - high.astype(F32)).astype(BF16)


def parity():
    return lax.rem(lax.axis_index("dev"), 2)


def columns(count):
    return [slice(LANES * j, LANES * (j + 1)) for j in range(count)]


def pack_kernel(live, fluxes, target, source, margin, edge, pair, weight):
    rounds, slots = target.shape
    fields, cells = fluxes.shape
    odd = parity() == 1
    low = fluxes[:, 0:LANES]
    high = fluxes[:, cells - LANES : cells]
    edge[...] = jnp.where(odd, high, low)
    pair[0:rounds, :] = target[...].astype(F32)
    pair[rounds : 2 * rounds, :] = source[...].astype(F32)
    lane = lax.broadcasted_iota(I32, (1, slots), 1)
    for r in range(rounds):
        weight[r : r + 1, :] = jnp.where(lane < live[0, r], margin[r : r + 1, :], 0.0)
    pair[2 * rounds : 3 * rounds, :] = weight[...]
    pair[3 * rounds : 3 * rounds + fields, 0:LANES] = jnp.where(odd, low, high)


def gradient_block(j, table_of, fluxes, neighbours, coef, grads):
    fields = fluxes.shape[0]
    cols = slice(LANES * j, LANES * (j + 1))
    picks = []
    for k in range(neighbours.shape[0]):
        spot = neighbours[k : k + 1, cols] + (LANES - HALO - LANES * j)
        place = lax.shift_right_logical(spot, 7)
        picks.append((spread(place == 1), spread(place == 2), spread(spot & (LANES - 1))))
    for g in range(fields // SUB):
        rows = slice(SUB * g, SUB * (g + 1))
        mine = fluxes[rows, cols]
        tables = [table_of(j + step, rows) for step in (-1, 0, 1)]
        zero = jnp.zeros((SUB, LANES), F32)
        one = jnp.zeros((SUB, LANES), F32)
        for k, (middle, last, lane) in enumerate(picks):
            got = take_lanes(tables[0], lane)
            got = jnp.where(middle, take_lanes(tables[1], lane), got)
            got = jnp.where(last, take_lanes(tables[2], lane), got)
            differ = got - mine
            zero = zero + spread(coef[k, 0:1, cols]) * differ
            one = one + spread(coef[k, 1:2, cols]) * differ
        grads[0, rows, cols] = zero
        grads[1, rows, cols] = one


def rounds_of_block(b, rounds):
    half = rounds // 2
    if b < half:
        return 2 * b, 2 * b
    other = 2 * (b - half)
    return other + 1, other - 1 if other else rounds - 1


def pick(ref, spots, is_odd, lead=()):
    rounds = ref.shape[-2]
    even, odd = [min(max(r, 0), rounds - 1) for r in spots]
    if even == odd:
        return ref[(*lead, slice(even, even + 1), slice(None))]
    return jnp.where(is_odd, ref[(*lead, slice(odd, odd + 1), slice(None))], ref[(*lead, slice(even, even + 1), slice(None))])


def inner_kernel(fluxes, neighbours, coef, source, shift, target, sea, part, temps, grads, spots, shifts):
    fields, cells = fluxes.shape
    rounds, slots = source.shape
    cell_cols = cells // LANES
    is_odd = parity() == 1
    for b in range(rounds):
        pair_of = rounds_of_block(b, rounds)
        spots[b] = spread(pick(source, pair_of, is_odd))
        for i in range(2):
            shifts[i, b] = spread(pick(shift, pair_of, is_odd, (i,)))
    own = lambda j, rows: fluxes[rows, LANES * j : LANES * (j + 1)]
    for j in range(1, cell_cols - 1):
        gradient_block(j, own, fluxes, neighbours, coef, grads)

    @pl.loop(0, rounds)
    def _(b):
        for c in range(slots // LANES):
            cols = slice(LANES * c, LANES * (c + 1))
            spot = spots[b, :, cols]
            place = lax.shift_right_logical(spot, 7)
            lane = spot & (LANES - 1)
            d0 = shifts[0, b, :, cols]
            d1 = shifts[1, b, :, cols]
            for g in range(fields // SUB):
                rows = slice(SUB * g, SUB * (g + 1))
                f = g0 = g1 = jnp.zeros((SUB, LANES), F32)
                for j in range(1, cell_cols - 1):
                    src = slice(LANES * j, LANES * (j + 1))
                    hit = place == j
                    f = jnp.where(hit, take_lanes(fluxes[rows, src], lane), f)
                    g0 = jnp.where(hit, take_lanes(grads[0, rows, src], lane), g0)
                    g1 = jnp.where(hit, take_lanes(grads[1, rows, src], lane), g1)
                part[b, rows, cols] = f + d0 * g0 + d1 * g1

    for top in range(0, rounds, SUB):
        for c in range(slots // LANES):
            cols = slice(LANES * c, LANES * (c + 1))
            spot = target[top : top + SUB, cols]
            place = lax.shift_right_logical(spot, 7)
            lane = spot & (LANES - 1)
            total = jnp.zeros((SUB, LANES), F32)
            for j in range(sea.shape[1] // LANES):
                table = spread(sea[:, LANES * j : LANES * (j + 1)])
                total = jnp.where(place == j, take_lanes(table, lane), total)
            temps[top : top + SUB, cols] = total


def outer_kernel(fluxes, neighbours, coef, source, shift, weight, part, temps, edge, pair, *rest):
    fields, cells = fluxes.shape
    rounds, slots = source.shape
    half = rounds // 2
    quarter = rounds // 4
    cell_cols = cells // LANES
    outs, grads = rest[:-1], rest[-1]
    steps = [m for m in range(-quarter, quarter + 1)]
    sends = dict(zip(steps, outs))
    is_odd = parity() == 1
    pair_edge = lambda rows: pair[3 * rounds + rows.start : 3 * rounds + rows.stop, 0:LANES]

    def table_of(j, rows):
        if j < 0:
            return jnp.where(is_odd, pair_edge(rows), edge[rows, :])
        if j >= cell_cols:
            return jnp.where(is_odd, edge[rows, :], pair_edge(rows))
        return fluxes[rows, LANES * j : LANES * (j + 1)]

    ends = (0, cell_cols - 1)
    for j in ends:
        gradient_block(j, table_of, fluxes, neighbours, coef, grads)

    for b in range(rounds):
        if b < half:
            spots = [(b - quarter, 0)]
        elif b == half:
            spots = [(-quarter, fields), (quarter, 0)]
        else:
            spots = [(b - half - quarter, fields)]
        pair_of = rounds_of_block(b, rounds)
        rows_of = [pick(source, pair_of, is_odd), pick(weight, pair_of, is_odd)]
        rows_of += [pick(shift, pair_of, is_odd, (i,)) for i in range(2)]
        for c in range(slots // LANES):
            cols = slice(LANES * c, LANES * (c + 1))
            spot, w, d0, d1 = [spread(row[:, cols]) for row in rows_of]
            place = lax.shift_right_logical(spot, 7)
            lane = spot & (LANES - 1)
            for g in range(fields // SUB):
                rows = slice(SUB * g, SUB * (g + 1))
                total = part[b, rows, cols]
                for j in ends:
                    src = slice(LANES * j, LANES * (j + 1))
                    got = (
                        take_lanes(fluxes[rows, src], lane)
                        + d0 * take_lanes(grads[0, rows, src], lane)
                        + d1 * take_lanes(grads[1, rows, src], lane)
                    )
                    total = jnp.where(place == j, got, total)
                for m, base in spots:
                    sends[m][base + SUB * g : base + SUB * (g + 1), cols] = w * total

    for m in steps:
        base = fields if m == quarter else 2 * fields
        r = -2 * m + half
        sends[m][base : base + 1, :] = pick(temps, (r, r), is_odd)
        sends[m][base + 1 : base + 2, :] = pick(temps, (r - 1, r + 1), is_odd)
        sends[m][base + 2 : base + SUB, :] = jnp.zeros((SUB - 2, slots), F32)


def scatter_kernel(target, source, weight, pair, *rest):
    rounds, slots = target.shape
    half = rounds // 2
    quarter = rounds // 4
    steps = [m for m in range(-quarter, quarter + 1)]
    blocks = dict(zip(steps, rest[: len(steps)]))
    mine, mine_sst, theirs = rest[len(steps) :]
    fields, ocean = mine.shape
    atmos = mine_sst.shape[1]
    is_odd = parity() == 1
    ocean_tiles = ocean // WIDE
    atmos_tiles = atmos // WIDE
    iota = lax.broadcasted_iota(I32, (WIDE, slots), 0)
    tile_row = lax.broadcasted_iota(I32, (SUB, slots), 0)

    def one_hot(spot):
        return jnp.where(spread(spot & (WIDE - 1), WIDE) == iota, 1.0, 0.0).astype(BF16)

    def add_ocean(acc, value, spot):
        tile = lax.shift_right_logical(spot, 8)
        high, low = halves(value)
        both = jnp.concatenate([high, low], axis=0).astype(F32)
        parts = [jnp.where(spread(tile, 2 * fields) == a, both, 0.0).astype(BF16) for a in range(ocean_tiles)]
        return acc + on_mxu(jnp.concatenate(parts, axis=0), one_hot(spot))

    def add_atmos(acc, value, spot):
        tile = spread(lax.shift_right_logical(spot, 8))
        high, low = halves(value)
        parts = [jnp.where(tile == tile_row, spread(x.astype(F32)), 0.0) for x in (high, low)]
        return acc + on_mxu(jnp.concatenate(parts, axis=0).astype(BF16), one_hot(spot))

    twin_target, twin_source, twin_weight = [pair.at[rounds * i : rounds * (i + 1)] for i in range(3)]
    acc = [jnp.zeros((ocean_tiles * 2 * fields, WIDE), F32) for _ in range(2)]
    sst = [jnp.zeros((2 * SUB, WIDE), F32) for _ in range(2)]
    for m in steps:
        ref = blocks[m]
        if m < quarter:
            r = 2 * m + half
            acc[0] = add_ocean(acc[0], ref[0:fields, :], target[r : r + 1, :])
        if m == -quarter:
            value = jnp.where(is_odd, blocks[quarter][0:fields, :], ref[fields : 2 * fields, :])
            spots = (1, rounds - 1)
        elif m < quarter:
            value = ref[fields : 2 * fields, :]
            spots = (2 * m + half + 1, 2 * m + half - 1)
        if m < quarter:
            acc[1] = add_ocean(acc[1], value, pick(twin_target, spots, is_odd).astype(I32))
        base = fields if m == quarter else 2 * fields
        if m > -quarter:
            r = -2 * m + half
            sst[0] = add_atmos(sst[0], ref[base : base + 1, :] * weight[r : r + 1, :], source[r : r + 1, :])
        spots = (-2 * m + half - 1, -2 * m + half + 1)
        value = ref[base + 1 : base + 2, :] * pick(twin_weight, spots, is_odd)
        if m == -quarter:
            value = jnp.where(is_odd, 0.0, value)
        if m == quarter:
            value = jnp.where(is_odd, value, 0.0)
        sst[1] = add_atmos(sst[1], value, pick(twin_source, spots, is_odd).astype(I32))
    for a in range(ocean_tiles):
        cols = slice(WIDE * a, WIDE * (a + 1))
        top = 2 * fields * a
        mine[:, cols] = acc[0][top : top + fields] + acc[0][top + fields : top + 2 * fields]
        theirs[0:fields, cols] = acc[1][top : top + fields] + acc[1][top + fields : top + 2 * fields]
    sums = [x[0:SUB] + x[SUB : 2 * SUB] for x in sst]
    theirs[fields : fields + SUB, :] = jnp.zeros((SUB, ocean), F32)
    theirs[fields : fields + SUB, 0:WIDE] = sums[1]
    for a in range(atmos_tiles):
        cols = slice(WIDE * a, WIDE * (a + 1))
        mine_sst[:, cols] = sums[0][a : a + 1]


def close_kernel(mine, mine_sst, moved, ocean_area, atmos_area, ocean_out, atmos_out):
    fields = mine.shape[0]
    ocean_out[...] = (mine[...] + moved[0:fields, :]) / ocean_area[...]
    for a in range(mine_sst.shape[1] // WIDE):
        cols = slice(WIDE * a, WIDE * (a + 1))
        both = mine_sst[:, cols] + moved[fields + a : fields + a + 1, 0:WIDE]
        atmos_out[:, cols] = both / atmos_area[:, cols]


def shards(
    fluxes,
    neighbours,
    grad_coef,
    source_cell,
    displacement,
    margin_weight,
    live_count,
    target_cell,
    ocean_area,
    sea_temp,
    atmos_area,
):
    fields, cells = fluxes.shape
    rounds, slots = source_cell.shape
    ocean = ocean_area.shape[0]
    count = lax.axis_size("dev")
    quarter = rounds // 4
    shape = lambda *dims: jax.ShapeDtypeStruct(dims, F32)
    whole = pl.BlockSpec(memory_space=pltpu.VMEM)
    scalar = pl.BlockSpec(memory_space=pltpu.SMEM)

    def call(kernel, outs, name, scratch=(), scalars=0):
        def run(*args):
            specs = [scalar] * scalars + [whole] * (len(args) - scalars)
            return pl.pallas_call(
                kernel,
                out_shape=outs,
                in_specs=specs,
                out_specs=[whole] * len(outs),
                scratch_shapes=list(scratch),
                name=name,
            )(*args)

        return run

    edge, pair, weight = call(
        pack_kernel,
        [shape(fields, LANES), shape(3 * rounds + fields, slots), shape(rounds, slots)],
        "pack",
        scalars=1,
    )(live_count, fluxes, target_cell, source_cell, margin_weight)
    rim = [(q, (q + 1) % count if q % 2 else (q - 1) % count) for q in range(count)]
    twin = [(q, q ^ 1) for q in range(count)]
    edge = lax.ppermute(edge, "dev", rim)
    pair = lax.ppermute(pair, "dev", twin)
    part, temps, grads = call(
        inner_kernel,
        [shape(rounds, fields, slots), shape(rounds, slots), shape(2, fields, cells)],
        "inner",
        scratch=[pltpu.VMEM((rounds, SUB, slots), I32), pltpu.VMEM((2, rounds, SUB, slots), F32)],
    )(fluxes, neighbours, grad_coef, source_cell, displacement, target_cell, sea_temp.reshape(1, -1))
    steps = [m for m in range(-quarter, quarter + 1)]
    tall = lambda m: (fields if m == quarter else 2 * fields) + SUB
    blocks = call(
        outer_kernel,
        [shape(tall(m), slots) for m in steps],
        "outer",
        scratch=[pltpu.VMEM((2, fields, cells), F32)],
    )(fluxes, neighbours, grad_coef, source_cell, displacement, weight, part, temps, edge, pair)
    blocks = dict(zip(steps, blocks))
    order = [m for m in (-4, -2, -1, -3, 1, 3, 2, 4)] if quarter == 4 else [m for m in steps if m]
    for m in order:
        pairs = [(q, (q + 2 * m) % count) for q in range(count)]
        blocks[m] = lax.ppermute(blocks[m], "dev", pairs)
    mine, mine_sst, theirs = call(
        scatter_kernel,
        [shape(fields, ocean), shape(1, cells), shape(fields + SUB, ocean)],
        "scatter",
    )(target_cell, source_cell, weight, pair, *[blocks[m] for m in steps])
    moved = lax.ppermute(theirs, "dev", twin)
    ocean_flux, atmos = call(
        close_kernel,
        [shape(fields, ocean), shape(1, cells)],
        "close",
    )(mine, mine_sst, moved, ocean_area.reshape(1, -1), atmos_area.reshape(1, -1))
    return ocean_flux, atmos.reshape(-1)


def solution(mesh):
    in_specs = (
        P(None, "dev"),
        P(None, "dev"),
        P(None, None, "dev"),
        P(None, "dev"),
        P(None, None, "dev"),
        P(None, "dev"),
        P("dev", None),
        P(None, "dev"),
        P("dev"),
        P("dev"),
        P("dev"),
    )
    out_specs = (P(None, "dev"), P("dev"))
    return jax.shard_map(shards, mesh=mesh, in_specs=in_specs, out_specs=out_specs, check_vma=False)
```

```python
import functools

import jax
import jax.numpy as jnp
from jax import lax
from jax.experimental import pallas as pl
from jax.experimental.pallas import tpu as pltpu
from jax.sharding import PartitionSpec as P

HALO = 96
LANES = 128
SUB = 8
WIDE = 256
F32 = jnp.float32
I32 = jnp.int32
BF16 = jnp.bfloat16


def take_lanes(table, lane):
    return jnp.take_along_axis(table, lane, axis=1, mode="promise_in_bounds")


def spread(row, count=SUB):
    return jnp.broadcast_to(row, (count, row.shape[1]))


def on_mxu(a, b):
    return lax.dot_general(a, b, (((1,), (1,)), ((), ())), preferred_element_type=F32)


def halves(x):
    high = x.astype(BF16)
    return jnp.concatenate([high, (x - high.astype(F32)).astype(BF16)], axis=0)


def one_hot(spot, base, count):
    near = jnp.broadcast_to((spot - base).astype(F32).astype(BF16), (count, spot.shape[1]))
    rows = lax.broadcasted_iota(I32, (count, spot.shape[1]), 0).astype(F32).astype(BF16)
    return jnp.where(near == rows, jnp.ones((), BF16), jnp.zeros((), BF16))


def parity():
    return lax.rem(lax.axis_index("dev"), 2)


def pack_kernel(live, first, final, target, source, margin, edge, pair, weight):
    rounds, slots = target.shape
    fields = first.shape[0]
    odd = parity() == 1
    low = first[...]
    high = final[...]
    edge[...] = jnp.where(odd, high, low)
    pair[0:rounds, :] = target[...].astype(F32)
    pair[rounds : 2 * rounds, :] = source[...].astype(F32)
    lane = lax.broadcasted_iota(I32, (1, slots), 1)
    for r in range(rounds):
        weight[r : r + 1, :] = jnp.where(lane < live[0, r], margin[r : r + 1, :], 0.0)
    pair[2 * rounds : 3 * rounds, :] = weight[...]
    pair[3 * rounds : 3 * rounds + fields, 0:LANES] = jnp.where(odd, low, high)


def gradient_block(j, table_of, fluxes, neighbours, coef, grads):
    fields = fluxes.shape[0]
    cols = slice(LANES * j, LANES * (j + 1))
    picks = []
    for k in range(neighbours.shape[0]):
        spot = neighbours[k : k + 1, cols] + (LANES - HALO - LANES * j)
        place = lax.shift_right_logical(spot, 7)
        picks.append((spread(place == 1), spread(place == 2), spread(spot & (LANES - 1))))
    for g in range(fields // SUB):
        rows = slice(SUB * g, SUB * (g + 1))
        mine = fluxes[rows, cols]
        tables = [table_of(j + step, rows) for step in (-1, 0, 1)]
        zero = jnp.zeros((SUB, LANES), F32)
        one = jnp.zeros((SUB, LANES), F32)
        for k, (middle, last, lane) in enumerate(picks):
            got = take_lanes(tables[0], lane)
            got = jnp.where(middle, take_lanes(tables[1], lane), got)
            got = jnp.where(last, take_lanes(tables[2], lane), got)
            differ = got - mine
            zero = zero + spread(coef[k, 0:1, cols]) * differ
            one = one + spread(coef[k, 1:2, cols]) * differ
        grads[0, rows, cols] = zero
        grads[1, rows, cols] = one


def rounds_of_block(b, rounds):
    half = rounds // 2
    if b < half:
        return 2 * b, 2 * b
    other = 2 * (b - half)
    return other + 1, other - 1 if other else rounds - 1


def pick(ref, spots, is_odd, lead=()):
    rounds = ref.shape[-2]
    even, odd = [min(max(r, 0), rounds - 1) for r in spots]
    if even == odd:
        return ref[(*lead, slice(even, even + 1), slice(None))]
    return jnp.where(is_odd, ref[(*lead, slice(odd, odd + 1), slice(None))], ref[(*lead, slice(even, even + 1), slice(None))])


def inner_kernel(fluxes, neighbours, coef, source, shift, target, weight, sea, part, temps, grads, tables, rows_of):
    fields, cells = fluxes.shape
    rounds, slots = source.shape
    cell_cols = cells // LANES
    is_odd = parity() == 1
    for b in range(rounds):
        pair_of = rounds_of_block(b, rounds)
        w = pick(weight, pair_of, is_odd)
        rows_of[b, 0:1] = pick(source, pair_of, is_odd).astype(F32)
        rows_of[b, 1:2] = w
        for i in range(2):
            rows_of[b, 2 + i : 3 + i] = w * pick(shift, pair_of, is_odd, (i,))
    own = lambda j, rows: fluxes[rows, LANES * j : LANES * (j + 1)]
    for j in range(1, cell_cols - 1):
        gradient_block(j, own, fluxes, neighbours, coef, grads)
    tables[0 : 2 * fields, :] = halves(fluxes[...])
    for j in (0, cell_cols - 1):
        cols = slice(LANES * j, LANES * (j + 1))
        tables[2 * fields : 6 * fields, cols] = jnp.zeros((4 * fields, LANES), BF16)
    mid = slice(LANES, cells - LANES)
    for i in range(2):
        tables[2 * fields * (i + 1) : 2 * fields * (i + 2), mid] = halves(grads[i, :, mid])

    @pl.loop(0, rounds)
    def _(b):
        spot = rows_of[b, 0:1].astype(I32)
        total = None
        for base in range(0, cells, WIDE):
            count = min(WIDE, cells - base)
            got = lax.dot_general(
                tables[:, base : base + count],
                one_hot(spot, base, count),
                (((1,), (0,)), ((), ())),
                preferred_element_type=F32,
            )
            total = got if total is None else total + got
        parts = [total[2 * fields * i : 2 * fields * i + fields] + total[2 * fields * i + fields : 2 * fields * (i + 1)] for i in range(3)]
        part[b] = sum(spread(rows_of[b, 1 + i : 2 + i], fields) * parts[i] for i in range(3))

    for top in range(0, rounds, SUB):
        for c in range(slots // LANES):
            cols = slice(LANES * c, LANES * (c + 1))
            spot = target[top : top + SUB, cols]
            place = lax.shift_right_logical(spot, 7)
            lane = spot & (LANES - 1)
            total = jnp.zeros((SUB, LANES), F32)
            for j in range(sea.shape[0] // LANES):
                table = spread(sea[pl.ds(LANES * j, LANES)][None, :])
                total = jnp.where(place == j, take_lanes(table, lane), total)
            temps[top : top + SUB, cols] = total


def outer_kernel(fluxes, neighbours, coef, source, shift, weight, part, temps, edge, pair, *rest):
    fields, cells = fluxes.shape
    rounds, slots = source.shape
    half = rounds // 2
    quarter = rounds // 4
    cell_cols = cells // LANES
    outs, grads = rest[:-1], rest[-1]
    steps = [m for m in range(-quarter, quarter + 1)]
    sends = dict(zip(steps, outs))
    is_odd = parity() == 1
    pair_edge = lambda rows: pair[3 * rounds + rows.start : 3 * rounds + rows.stop, 0:LANES]

    def table_of(j, rows):
        if j < 0:
            return jnp.where(is_odd, pair_edge(rows), edge[rows, :])
        if j >= cell_cols:
            return jnp.where(is_odd, edge[rows, :], pair_edge(rows))
        return fluxes[rows, LANES * j : LANES * (j + 1)]

    ends = (0, cell_cols - 1)
    for j in ends:
        gradient_block(j, table_of, fluxes, neighbours, coef, grads)

    for b in range(rounds):
        if b < half:
            spots = [(b - quarter, 0)]
        elif b == half:
            spots = [(-quarter, fields), (quarter, 0)]
        else:
            spots = [(b - half - quarter, fields)]
        pair_of = rounds_of_block(b, rounds)
        rows_of = [pick(source, pair_of, is_odd), pick(weight, pair_of, is_odd)]
        rows_of += [pick(shift, pair_of, is_odd, (i,)) for i in range(2)]
        for c in range(slots // LANES):
            cols = slice(LANES * c, LANES * (c + 1))
            spot, w, d0, d1 = [row[:, cols] for row in rows_of]
            place = lax.shift_right_logical(spot, 7)
            at_end = jnp.logical_or(place == ends[0], place == ends[1])
            w = jnp.where(at_end, w, 0.0)
            d = [spread(w * d0), spread(w * d1)]
            place = spread(place)
            lane = spread(spot & (LANES - 1))
            for g in range(fields // SUB):
                rows = slice(SUB * g, SUB * (g + 1))
                total = part[b, rows, cols]
                for i in range(2):
                    got = [take_lanes(grads[i, rows, LANES * j : LANES * (j + 1)], lane) for j in ends]
                    total = total + d[i] * jnp.where(place == ends[0], got[0], got[1])
                for m, base in spots:
                    sends[m][base + SUB * g : base + SUB * (g + 1), cols] = total

    for m in steps:
        base = fields if m == quarter else 2 * fields
        r = -2 * m + half
        sends[m][base : base + 1, :] = pick(temps, (r, r), is_odd)
        sends[m][base + 1 : base + 2, :] = pick(temps, (r - 1, r + 1), is_odd)
        sends[m][base + 2 : base + SUB, :] = jnp.zeros((SUB - 2, slots), F32)


def scatter(sums, blocks, steps, edge_block, refs, rounds, fields, tiles, is_odd):
    target, source, weight, pair = refs
    half = rounds // 2
    quarter = rounds // 4
    slots = target.shape[1]
    twin_target, twin_source, twin_weight = [pair.at[rounds * i : rounds * (i + 1)] for i in range(3)]
    acc, sst = sums
    tile_row = lax.broadcasted_iota(I32, (2 * SUB, slots), 0).astype(F32).astype(BF16)
    zero = jnp.zeros((), BF16)

    def tile_of(spot, count):
        return jnp.broadcast_to(lax.shift_right_logical(spot, 8).astype(F32).astype(BF16), (count, slots))

    def add_ocean(acc, value, spot):
        tile = tile_of(spot, 2 * fields)
        both = halves(value)
        parts = [jnp.where(tile == jnp.array(a, BF16), both, zero) for a in range(tiles)]
        return acc + on_mxu(jnp.concatenate(parts, axis=0), one_hot(spot & (WIDE - 1), 0, WIDE))

    def add_atmos(acc, value, spot):
        tile = tile_of(spot, 2 * SUB)
        both = halves(value)
        high = jnp.broadcast_to(both[0:1], (2 * SUB, slots))
        low = jnp.broadcast_to(both[1:2], (2 * SUB, slots))
        lhs = jnp.concatenate([jnp.where(tile == tile_row, x, zero) for x in (high, low)], axis=0)
        return acc + on_mxu(lhs, one_hot(spot & (WIDE - 1), 0, WIDE))

    for m in steps:
        ref = blocks[m]
        if m < quarter:
            r = 2 * m + half
            acc[0] = add_ocean(acc[0], ref[0:fields, :], target[r : r + 1, :])
        if -quarter < m < quarter:
            spots = (2 * m + half + 1, 2 * m + half - 1)
            acc[1] = add_ocean(acc[1], ref[fields : 2 * fields, :], pick(twin_target, spots, is_odd).astype(I32))
        base = fields if m == quarter else 2 * fields
        if m > -quarter:
            r = -2 * m + half
            sst[0] = add_atmos(sst[0], ref[base : base + 1, :] * weight[r : r + 1, :], source[r : r + 1, :])
        spots = (-2 * m + half - 1, -2 * m + half + 1)
        value = ref[base + 1 : base + 2, :] * pick(twin_weight, spots, is_odd)
        if m == -quarter:
            value = jnp.where(is_odd, 0.0, value)
        if m == quarter:
            value = jnp.where(is_odd, value, 0.0)
        sst[1] = add_atmos(sst[1], value, pick(twin_source, spots, is_odd).astype(I32))
    if edge_block:
        value = jnp.where(is_odd, blocks[quarter][0:fields, :], blocks[-quarter][fields : 2 * fields, :])
        acc[1] = add_ocean(acc[1], value, pick(twin_target, (1, rounds - 1), is_odd).astype(I32))


def scatter_kernel(steps, fresh, final, target, source, weight, pair, *rest):
    rounds = target.shape[0]
    quarter = rounds // 4
    held = list(steps) + ([-quarter] if final and -quarter not in steps else [])
    blocks = dict(zip(held, rest[: len(held)]))
    carry, (mine, mine_sst, theirs) = rest[len(held) : -3], rest[-3:]
    fields, ocean = mine.shape
    tiles = ocean // WIDE
    is_odd = parity() == 1
    acc = [jnp.zeros((tiles * 2 * fields, WIDE), F32) for _ in range(2)]
    sst = [jnp.zeros((4 * SUB, WIDE), F32) for _ in range(2)]
    scatter((acc, sst), blocks, steps, final, (target, source, weight, pair), rounds, fields, tiles, is_odd)
    for a in range(tiles):
        cols = slice(WIDE * a, WIDE * (a + 1))
        top = 2 * fields * a
        own, other = [x[top : top + fields] + x[top + fields : top + 2 * fields] for x in acc]
        if not fresh:
            own = own + carry[0][:, cols]
            other = other + carry[2][0:fields, cols]
        mine[:, cols] = own
        theirs[0:fields, cols] = other
    own, other = [x[0:SUB] + x[2 * SUB : 3 * SUB] for x in sst]
    if not fresh:
        own = own + carry[1][...]
        other = other + carry[2][fields : fields + SUB, 0:WIDE]
    mine_sst[...] = own
    theirs[fields : fields + SUB, :] = jnp.zeros((SUB, ocean), F32)
    theirs[fields : fields + SUB, 0:WIDE] = other


def close_kernel(mine, mine_sst, moved, ocean_area, atmos_area, ocean_out, atmos_out):
    fields, ocean = mine.shape
    for j in range(ocean // LANES):
        cols = slice(LANES * j, LANES * (j + 1))
        area = spread(ocean_area[pl.ds(LANES * j, LANES)][None, :], fields)
        ocean_out[:, cols] = (mine[:, cols] + moved[0:fields, cols]) / area
    for j in range(atmos_area.shape[0] // LANES):
        a, side = j // 2, LANES * (j % 2)
        both = mine_sst[a : a + 1, side : side + LANES] + moved[fields + a : fields + a + 1, side : side + LANES]
        atmos_out[pl.ds(LANES * j, LANES)] = (both / atmos_area[pl.ds(LANES * j, LANES)][None, :])[0]


def shards(
    fluxes,
    neighbours,
    grad_coef,
    source_cell,
    displacement,
    margin_weight,
    live_count,
    target_cell,
    ocean_area,
    sea_temp,
    atmos_area,
):
    fields, cells = fluxes.shape
    rounds, slots = source_cell.shape
    ocean = ocean_area.shape[0]
    count = lax.axis_size("dev")
    quarter = rounds // 4
    shape = lambda *dims: pltpu.VMEM(dims, F32)
    whole = pl.BlockSpec(memory_space=pltpu.VMEM)
    scalar = pl.BlockSpec(memory_space=pltpu.SMEM)
    near = lambda x: pltpu.with_memory_space_constraint(x, pltpu.VMEM)

    def call(kernel, outs, name, specs, args, scratch=(), grid=()):
        return pl.pallas_call(
            kernel,
            out_shape=outs,
            in_specs=specs,
            out_specs=[whole] * len(outs),
            scratch_shapes=list(scratch),
            grid=grid,
            name=name,
        )(*args)

    edge_spec = lambda at: pl.BlockSpec((fields, LANES), lambda i: (0, at))
    edge, pair, weight = call(
        pack_kernel,
        [shape(fields, LANES), shape(3 * rounds + fields, slots), shape(rounds, slots)],
        "pack",
        [scalar, edge_spec(0), edge_spec(cells // LANES - 1), whole, whole, whole],
        (live_count, fluxes, fluxes, target_cell, source_cell, margin_weight),
        grid=(1,),
    )
    rim = [(q, (q + 1) % count if q % 2 else (q - 1) % count) for q in range(count)]
    twin = [(q, q ^ 1) for q in range(count)]
    edge = near(lax.ppermute(edge, "dev", rim))
    pair = near(lax.ppermute(pair, "dev", twin))
    cell_args = [near(x) for x in (fluxes, neighbours, grad_coef, source_cell, displacement)]
    target_near = near(target_cell)
    source_near = cell_args[3]
    weight = near(weight)
    args = (*cell_args, target_near, weight, near(sea_temp))
    part, temps = call(
        inner_kernel,
        [shape(rounds, fields, slots), shape(rounds, slots)],
        "inner",
        [whole] * len(args),
        args,
        scratch=[
            pltpu.VMEM((2, fields, cells), F32),
            pltpu.VMEM((6 * fields, cells), BF16),
            pltpu.VMEM((rounds, SUB, slots), F32),
        ],
    )
    steps = [m for m in range(-quarter, quarter + 1)]
    tall = lambda m: (fields if m == quarter else 2 * fields) + SUB
    args = (*cell_args, weight, near(part), near(temps), edge, pair)
    blocks = call(
        outer_kernel,
        [shape(tall(m), slots) for m in steps],
        "outer",
        [whole] * len(args),
        args,
        scratch=[pltpu.VMEM((2, fields, cells), F32)],
    )
    blocks = {m: near(x) for m, x in zip(steps, blocks)}
    order = [m for m in steps if m]
    for m in order:
        pairs = [(q, (q + 2 * m) % count) for q in range(count)]
        blocks[m] = near(lax.ppermute(blocks[m], "dev", pairs))
    sums = ()
    groups = [[0] + order[:5], order[5:]]
    for i, group in enumerate(groups):
        final = i == len(groups) - 1
        held = group + ([-quarter] if final and -quarter not in group else [])
        args = (target_near, source_near, weight, pair, *[blocks[m] for m in held], *[near(x) for x in sums])
        sums = call(
            functools.partial(scatter_kernel, tuple(group), i == 0, final),
            [shape(fields, ocean), shape(SUB, WIDE), shape(fields + SUB, ocean)],
            "scatter",
            [whole] * len(args),
            args,
        )
    mine, mine_sst, theirs = sums
    moved = near(lax.ppermute(theirs, "dev", twin))
    args = (near(mine), near(mine_sst), moved, near(ocean_area), near(atmos_area))
    return tuple(
        call(
            close_kernel,
            [jax.ShapeDtypeStruct((fields, ocean), F32), jax.ShapeDtypeStruct((cells,), F32)],
            "close",
            [whole] * len(args),
            args,
        )
    )


def solution(mesh):
    in_specs = (
        P(None, "dev"),
        P(None, "dev"),
        P(None, None, "dev"),
        P(None, "dev"),
        P(None, None, "dev"),
        P(None, "dev"),
        P("dev", None),
        P(None, "dev"),
        P("dev"),
        P("dev"),
        P("dev"),
    )
    out_specs = (P(None, "dev"), P("dev"))
    return jax.shard_map(shards, mesh=mesh, in_specs=in_specs, out_specs=out_specs, check_vma=False)
```

```python
import functools

import jax
import jax.numpy as jnp
from jax import lax
from jax.experimental import pallas as pl
from jax.experimental.pallas import tpu as pltpu
from jax.sharding import PartitionSpec as P

HALO = 96
LANES = 128
SUB = 8
WIDE = 256
F32 = jnp.float32
I32 = jnp.int32
BF16 = jnp.bfloat16


def take_lanes(table, lane):
    return jnp.take_along_axis(table, lane, axis=1, mode="promise_in_bounds")


def spread(row, count=SUB):
    return jnp.broadcast_to(row, (count, row.shape[1]))


def on_mxu(a, b):
    return lax.dot_general(a, b, (((1,), (1,)), ((), ())), preferred_element_type=F32)


def halves(x):
    high = x.astype(BF16)
    return jnp.concatenate([high, (x - high.astype(F32)).astype(BF16)], axis=0)


def one_hot(spot, base, count):
    near = jnp.broadcast_to((spot - base).astype(F32).astype(BF16), (count, spot.shape[1]))
    rows = lax.broadcasted_iota(I32, (count, spot.shape[1]), 0).astype(F32).astype(BF16)
    return jnp.where(near == rows, jnp.ones((), BF16), jnp.zeros((), BF16))


def parity():
    return lax.rem(lax.axis_index("dev"), 2)


def pack_kernel(live, first, final, target, source, margin, edge, pair, weight):
    rounds, slots = target.shape
    fields = first.shape[0]
    odd = parity() == 1
    low = first[...]
    high = final[...]
    edge[...] = jnp.where(odd, high, low)
    pair[0:rounds, :] = target[...].astype(F32)
    pair[rounds : 2 * rounds, :] = source[...].astype(F32)
    lane = lax.broadcasted_iota(I32, (1, slots), 1)
    for r in range(rounds):
        weight[r : r + 1, :] = jnp.where(lane < live[0, r], margin[r : r + 1, :], 0.0)
    pair[2 * rounds : 3 * rounds, :] = weight[...]
    pair[3 * rounds : 3 * rounds + fields, 0:LANES] = jnp.where(odd, low, high)


def gradient_block(j, table_of, fluxes, neighbours, coef, grads):
    fields = fluxes.shape[0]
    cols = slice(LANES * j, LANES * (j + 1))
    groups = [slice(SUB * g, SUB * (g + 1)) for g in range(fields // SUB)]
    zero = [jnp.zeros((SUB, LANES), F32) for _ in groups]
    one = [jnp.zeros((SUB, LANES), F32) for _ in groups]
    for k in range(neighbours.shape[0]):
        spot = neighbours[k : k + 1, cols] + (LANES - HALO - LANES * j)
        place = lax.shift_right_logical(spot, 7)
        middle, last, lane = spread(place == 1), spread(place == 2), spread(spot & (LANES - 1))
        c0, c1 = spread(coef[k, 0:1, cols]), spread(coef[k, 1:2, cols])
        for g, rows in enumerate(groups):
            got = [take_lanes(table_of(j + step, rows), lane) for step in (-1, 0, 1)]
            differ = jnp.where(last, got[2], jnp.where(middle, got[1], got[0])) - fluxes[rows, cols]
            zero[g] = zero[g] + c0 * differ
            one[g] = one[g] + c1 * differ
    for g, rows in enumerate(groups):
        grads[0, rows, cols] = zero[g]
        grads[1, rows, cols] = one[g]


def rounds_of_block(b, rounds):
    half = rounds // 2
    if b < half:
        return 2 * b, 2 * b
    other = 2 * (b - half)
    return other + 1, other - 1 if other else rounds - 1


def pick(ref, spots, is_odd, lead=()):
    rounds = ref.shape[-2]
    even, odd = [min(max(r, 0), rounds - 1) for r in spots]
    if even == odd:
        return ref[(*lead, slice(even, even + 1), slice(None))]
    return jnp.where(is_odd, ref[(*lead, slice(odd, odd + 1), slice(None))], ref[(*lead, slice(even, even + 1), slice(None))])


def spots_in_tiles(rounds, slots):
    for col in range(rounds * slots // LANES):
        b, c = divmod(col, slots // LANES)
        t, half = divmod(col, WIDE // LANES)
        yield t, slice(LANES * half, LANES * (half + 1)), b, slice(LANES * c, LANES * (c + 1))


def inner_kernel(fluxes, neighbours, coef, source, shift, target, weight, sea, part, temps, rows_of, grads, tables):
    fields, cells = fluxes.shape
    rounds, slots = source.shape
    cell_cols = cells // LANES
    is_odd = parity() == 1
    row = {}
    for b in range(rounds):
        pair_of = rounds_of_block(b, rounds)
        w = pick(weight, pair_of, is_odd)
        row[b] = [pick(source, pair_of, is_odd).astype(F32), w]
        row[b] += [w * pick(shift, pair_of, is_odd, (i,)) for i in range(2)]
    for t, to, b, cols in spots_in_tiles(rounds, slots):
        for i in range(4):
            rows_of[t, i : i + 1, to] = row[b][i][:, cols]
    own = lambda j, rows: fluxes[rows, LANES * j : LANES * (j + 1)]
    for j in range(1, cell_cols - 1):
        gradient_block(j, own, fluxes, neighbours, coef, grads)
    for j in (0, cell_cols - 1):
        grads[:, :, LANES * j : LANES * (j + 1)] = jnp.zeros((2, fields, LANES), F32)
    high = tables.shape[1]
    for a in range(cells // high):
        cols = slice(high * a, high * (a + 1))
        top = 6 * fields * a
        tables[top : top + 2 * fields, :] = halves(fluxes[:, cols])
        for i in range(2):
            at = top + 2 * fields * (i + 1)
            tables[at : at + 2 * fields, :] = halves(grads[i, :, cols])

    @pl.loop(0, part.shape[0])
    def _(t):
        spot = rows_of[t, 0:1].astype(I32)
        inside = lax.rem(spot, high)
        tile = spread(lax.div(spot, high), 6 * fields)
        total = None
        for base in range(0, high, WIDE):
            got = lax.dot_general(
                tables[:, base : base + WIDE],
                one_hot(inside, base, WIDE),
                (((1,), (0,)), ((), ())),
                preferred_element_type=F32,
            )
            total = got if total is None else total + got
        found = total[0 : 6 * fields]
        for a in range(1, cells // high):
            found = jnp.where(tile == a, total[6 * fields * a : 6 * fields * (a + 1)], found)
        parts = [found[2 * fields * i : 2 * fields * i + fields] + found[2 * fields * i + fields : 2 * fields * (i + 1)] for i in range(3)]
        scales = [spread(rows_of[t, 1 + i : 2 + i], fields) for i in range(3)]
        part[t] = scales[0] * parts[0] + (scales[1] * parts[1] + scales[2] * parts[2])

    for top in range(0, rounds, SUB):
        for c in range(slots // LANES):
            cols = slice(LANES * c, LANES * (c + 1))
            spot = target[top : top + SUB, cols]
            place = lax.shift_right_logical(spot, 7)
            lane = spot & (LANES - 1)
            total = jnp.zeros((SUB, LANES), F32)
            for j in range(sea.shape[0] // LANES):
                table = spread(sea[pl.ds(LANES * j, LANES)][None, :])
                total = jnp.where(place == j, take_lanes(table, lane), total)
            temps[top : top + SUB, cols] = total


def outer_kernel(fluxes, neighbours, coef, part, temps, rows_of, edge, pair, *rest):
    fields, cells = fluxes.shape
    rounds, slots = temps.shape
    half = rounds // 2
    quarter = rounds // 4
    cell_cols = cells // LANES
    outs, grads = rest[:-1], rest[-1]
    steps = [m for m in range(-quarter, quarter + 1)]
    sends = dict(zip(steps, outs))
    is_odd = parity() == 1
    pair_edge = lambda rows: pair[3 * rounds + rows.start : 3 * rounds + rows.stop, 0:LANES]

    def table_of(j, rows):
        if j < 0:
            return jnp.where(is_odd, pair_edge(rows), edge[rows, :])
        if j >= cell_cols:
            return jnp.where(is_odd, edge[rows, :], pair_edge(rows))
        return fluxes[rows, LANES * j : LANES * (j + 1)]

    ends = (0, cell_cols - 1)
    for j in ends:
        gradient_block(j, table_of, fluxes, neighbours, coef, grads)

    left = slice(0, LANES)
    right = slice(cells - LANES, cells)
    table = jnp.concatenate([halves(jnp.concatenate([grads[i, :, left], grads[i, :, right]], axis=1)) for i in range(2)], axis=0)
    places = {}
    for t, at, b, cols in spots_in_tiles(rounds, slots):
        places.setdefault(t, []).append((at, b, cols))
    for t in range(part.shape[0]):
        spot = rows_of[t, 0:1].astype(I32)
        end = jnp.where(spot < LANES, spot, jnp.where(spot < cells - LANES, 2 * WIDE, spot - (cells - WIDE)))
        got = lax.dot_general(table, one_hot(end, 0, WIDE), (((1,), (0,)), ((), ())), preferred_element_type=F32)
        parts = [got[2 * fields * i : 2 * fields * i + fields] + got[2 * fields * i + fields : 2 * fields * (i + 1)] for i in range(2)]
        scales = [spread(rows_of[t, 2 + i : 3 + i], fields) for i in range(2)]
        total = part[t] + (scales[0] * parts[0] + scales[1] * parts[1])
        for at, b, cols in places[t]:
            if b < half:
                spots = [(b - quarter, 0)]
            elif b == half:
                spots = [(-quarter, fields), (quarter, 0)]
            else:
                spots = [(b - half - quarter, fields)]
            for m, base in spots:
                sends[m][base : base + fields, cols] = total[:, at]

    for m in steps:
        base = fields if m == quarter else 2 * fields
        r = -2 * m + half
        sends[m][base : base + 1, :] = pick(temps, (r, r), is_odd)
        sends[m][base + 1 : base + 2, :] = pick(temps, (r - 1, r + 1), is_odd)
        sends[m][base + 2 : base + SUB, :] = jnp.zeros((SUB - 2, slots), F32)


def scatter(sums, blocks, steps, edge_block, refs, rounds, fields, tiles, is_odd):
    target, source, weight, pair = refs
    half = rounds // 2
    quarter = rounds // 4
    slots = target.shape[1]
    twin_target, twin_source, twin_weight = [pair.at[rounds * i : rounds * (i + 1)] for i in range(3)]
    tile_row = lax.broadcasted_iota(I32, (2 * SUB, slots), 0).astype(F32).astype(BF16)
    zero = jnp.zeros((), BF16)
    acc_in = ([], [])
    sst_in = ([], [])

    def tile_of(spot, shift, count):
        return jnp.broadcast_to(lax.shift_right_logical(spot, shift).astype(F32).astype(BF16), (count, slots))

    def add_ocean(into, value, spot):
        tile = tile_of(spot, 8, 2 * fields)
        both = halves(value)
        parts = [jnp.where(tile == jnp.array(a, BF16), both, zero) for a in range(tiles)]
        into.append((jnp.concatenate(parts, axis=0), one_hot(spot & (WIDE - 1), 0, WIDE)))

    def add_atmos(into, value, spot):
        tile = tile_of(spot, 7, 2 * SUB)
        both = halves(value)
        high = jnp.broadcast_to(both[0:1], (2 * SUB, slots))
        low = jnp.broadcast_to(both[1:2], (2 * SUB, slots))
        lhs = jnp.concatenate([jnp.where(tile == tile_row, x, zero) for x in (high, low)], axis=0)
        into.append((lhs, one_hot(spot & (LANES - 1), 0, LANES)))

    for m in steps:
        ref = blocks[m]
        if m < quarter:
            r = 2 * m + half
            add_ocean(acc_in[0], ref[0:fields, :], target[r : r + 1, :])
        if -quarter < m < quarter:
            spots = (2 * m + half + 1, 2 * m + half - 1)
            add_ocean(acc_in[1], ref[fields : 2 * fields, :], pick(twin_target, spots, is_odd).astype(I32))
        base = fields if m == quarter else 2 * fields
        if m > -quarter:
            r = -2 * m + half
            add_atmos(sst_in[0], ref[base : base + 1, :] * weight[r : r + 1, :], source[r : r + 1, :])
        spots = (-2 * m + half - 1, -2 * m + half + 1)
        value = ref[base + 1 : base + 2, :] * pick(twin_weight, spots, is_odd)
        if m == -quarter:
            value = jnp.where(is_odd, 0.0, value)
        if m == quarter:
            value = jnp.where(is_odd, value, 0.0)
        add_atmos(sst_in[1], value, pick(twin_source, spots, is_odd).astype(I32))
    if edge_block:
        value = jnp.where(is_odd, blocks[quarter][0:fields, :], blocks[-quarter][fields : 2 * fields, :])
        add_ocean(acc_in[1], value, pick(twin_target, (1, rounds - 1), is_odd).astype(I32))
    for sides, into in zip((acc_in, sst_in), sums):
        for i, terms in enumerate(sides):
            for at in range(0, len(terms), 2):
                lhs, rhs = [jnp.concatenate(x, axis=1) for x in zip(*terms[at : at + 2])]
                got = on_mxu(lhs, rhs)
                into[i] = got if into[i] is None else into[i] + got


def scatter_kernel(steps, fresh, final, target, source, weight, pair, *rest):
    rounds = target.shape[0]
    quarter = rounds // 4
    held = list(steps) + ([-quarter] if final and -quarter not in steps else [])
    blocks = dict(zip(held, rest[: len(held)]))
    carry, (mine, mine_sst, theirs) = rest[len(held) : -3], rest[-3:]
    fields, ocean = mine.shape
    tiles = ocean // WIDE
    is_odd = parity() == 1
    acc = [None, None]
    sst = [None, None]
    scatter((acc, sst), blocks, steps, final, (target, source, weight, pair), rounds, fields, tiles, is_odd)
    for a in range(tiles):
        cols = slice(WIDE * a, WIDE * (a + 1))
        top = 2 * fields * a
        own, other = [x[top : top + fields] + x[top + fields : top + 2 * fields] for x in acc]
        if not fresh:
            own = own + carry[0][:, cols]
            other = other + carry[2][0:fields, cols]
        mine[:, cols] = own
        theirs[0:fields, cols] = other
    own, other = [x[0 : 2 * SUB] + x[2 * SUB : 4 * SUB] for x in sst]
    if not fresh:
        own = own + carry[1][...]
        other = other + carry[2][fields : fields + 2 * SUB, 0:LANES]
    mine_sst[...] = own
    theirs[fields : fields + 2 * SUB, :] = jnp.zeros((2 * SUB, ocean), F32)
    theirs[fields : fields + 2 * SUB, 0:LANES] = other


def close_kernel(mine, mine_sst, moved, ocean_area, atmos_area, ocean_out, atmos_out):
    fields, ocean = mine.shape
    for j in range(ocean // LANES):
        cols = slice(LANES * j, LANES * (j + 1))
        area = spread(ocean_area[pl.ds(LANES * j, LANES)][None, :], fields)
        ocean_out[:, cols] = (mine[:, cols] + moved[0:fields, cols]) / area
    for j in range(atmos_area.shape[0] // LANES):
        both = mine_sst[j : j + 1, :] + moved[fields + j : fields + j + 1, 0:LANES]
        atmos_out[pl.ds(LANES * j, LANES)] = (both / atmos_area[pl.ds(LANES * j, LANES)][None, :])[0]


def shards(
    fluxes,
    neighbours,
    grad_coef,
    source_cell,
    displacement,
    margin_weight,
    live_count,
    target_cell,
    ocean_area,
    sea_temp,
    atmos_area,
):
    fields, cells = fluxes.shape
    rounds, slots = source_cell.shape
    ocean = ocean_area.shape[0]
    count = lax.axis_size("dev")
    quarter = rounds // 4
    shape = lambda *dims: pltpu.VMEM(dims, F32)
    whole = pl.BlockSpec(memory_space=pltpu.VMEM)
    scalar = pl.BlockSpec(memory_space=pltpu.SMEM)
    near = lambda x: pltpu.with_memory_space_constraint(x, pltpu.VMEM)

    def call(kernel, outs, name, specs, args, scratch=(), grid=()):
        return pl.pallas_call(
            kernel,
            out_shape=outs,
            in_specs=specs,
            out_specs=[whole] * len(outs),
            scratch_shapes=list(scratch),
            grid=grid,
            name=name,
        )(*args)

    edge_spec = lambda at: pl.BlockSpec((fields, LANES), lambda i: (0, at))
    edge, pair, weight = call(
        pack_kernel,
        [shape(fields, LANES), shape(3 * rounds + fields, slots), shape(rounds, slots)],
        "pack",
        [scalar, edge_spec(0), edge_spec(cells // LANES - 1), whole, whole, whole],
        (live_count, fluxes, fluxes, target_cell, source_cell, margin_weight),
        grid=(1,),
    )
    rim = [(q, (q + 1) % count if q % 2 else (q - 1) % count) for q in range(count)]
    twin = [(q, q ^ 1) for q in range(count)]
    edge = near(lax.ppermute(edge, "dev", rim))
    pair = near(lax.ppermute(pair, "dev", twin))
    cell_args = [near(x) for x in (fluxes, neighbours, grad_coef, source_cell, displacement)]
    target_near = near(target_cell)
    source_near = cell_args[3]
    weight = near(weight)
    args = (*cell_args, target_near, weight, near(sea_temp))
    tiles = rounds * slots // WIDE
    high = 2 * WIDE
    part, temps, rows_of = call(
        inner_kernel,
        [shape(tiles, fields, WIDE), shape(rounds, slots), shape(tiles, SUB, WIDE)],
        "inner",
        [whole] * len(args),
        args,
        scratch=[
            pltpu.VMEM((2, fields, cells), F32),
            pltpu.VMEM((6 * fields * (cells // high), high), BF16),
        ],
    )
    steps = [m for m in range(-quarter, quarter + 1)]
    tall = lambda m: (fields if m == quarter else 2 * fields) + SUB
    args = (*cell_args[:3], near(part), near(temps), near(rows_of), edge, pair)
    blocks = call(
        outer_kernel,
        [shape(tall(m), slots) for m in steps],
        "outer",
        [whole] * len(args),
        args,
        scratch=[pltpu.VMEM((2, fields, cells), F32)],
    )
    blocks = {m: near(x) for m, x in zip(steps, blocks)}
    order = [m for m in steps if m]
    for m in order:
        pairs = [(q, (q + 2 * m) % count) for q in range(count)]
        blocks[m] = near(lax.ppermute(blocks[m], "dev", pairs))
    sums = ()
    groups = [[0] + order[:5], order[5:]]
    for i, group in enumerate(groups):
        final = i == len(groups) - 1
        held = group + ([-quarter] if final and -quarter not in group else [])
        args = (target_near, source_near, weight, pair, *[blocks[m] for m in held], *[near(x) for x in sums])
        sums = call(
            functools.partial(scatter_kernel, tuple(group), i == 0, final),
            [shape(fields, ocean), shape(2 * SUB, LANES), shape(fields + 2 * SUB, ocean)],
            "scatter",
            [whole] * len(args),
            args,
        )
    mine, mine_sst, theirs = sums
    moved = near(lax.ppermute(theirs, "dev", twin))
    args = (near(mine), near(mine_sst), moved, near(ocean_area), near(atmos_area))
    return tuple(
        call(
            close_kernel,
            [jax.ShapeDtypeStruct((fields, ocean), F32), jax.ShapeDtypeStruct((cells,), F32)],
            "close",
            [whole] * len(args),
            args,
        )
    )


def solution(mesh):
    in_specs = (
        P(None, "dev"),
        P(None, "dev"),
        P(None, None, "dev"),
        P(None, "dev"),
        P(None, None, "dev"),
        P(None, "dev"),
        P("dev", None),
        P(None, "dev"),
        P("dev"),
        P("dev"),
        P("dev"),
    )
    out_specs = (P(None, "dev"), P("dev"))
    return jax.shard_map(shards, mesh=mesh, in_specs=in_specs, out_specs=out_specs, check_vma=False)
```
